32 devices in a mesh: rep: 4 (over y, x), shard: 8 (over z, core).
Axes of the slice: x: 2, y: 2, z: 4, core: 2. Of those that a mesh axis runs over, the one named last changes fastest.
Arguments:
- hidden: bfloat16 [32768, 768], P(('rep', 'shard')), may hold values from -6 to 6
- segment_ids: int32 [32, 1024], P(('rep', 'shard')), may hold values from 0 to 7, never falling along the last dimension, each value on 1 to 800 neighbouring positions
- cotangent: bfloat16 [32768, 768], P(('rep', 'shard'))
- w_query: bfloat16 [768, 384], P('shard'), may hold values from -0.21875 to 0.21875
- w_key: bfloat16 [768, 384], P('shard'), may hold values from -0.21875 to 0.21875
- w_value: bfloat16 [768, 384], P('shard'), may hold values from -0.21875 to 0.21875
- w_depth: bfloat16 [9, 768], P(None, 'shard'), may hold values from -2 to 2
- w_keyconv: bfloat16 [768, 384], P('shard'), may hold values from -0.21875 to 0.21875
- w_kernel: bfloat16 [54, 384], P(None, 'shard'), may hold values from -0.3125 to 0.3125
- w_convout: bfloat16 [768, 384], P('shard'), may hold values from -0.21875 to 0.21875
- w_output: bfloat16 [768, 768], P('shard'), may hold values from -0.875 to 0.875
- gain_attn: bfloat16 [768], P('shard'), may hold values from 0.5 to 1.5
- w_inter: bfloat16 [2, 384, 1536], P(None, None, 'shard'), may hold values from -0.3125 to 0.3125
- w_outer: bfloat16 [2, 1536, 384], P(None, 'shard'), may hold values from -0.15625 to 0.15625
- gain_ffn: bfloat16 [768], P('shard'), may hold values from 0.5 to 1.5
Outputs:
- output: bfloat16 [32768, 768], P(('rep', 'shard'))
- hidden_grad: float32 [32768, 768], P(('rep', 'shard'))
- grad_query: float32 [768, 384], P('shard')
- grad_key: float32 [768, 384], P('shard')
- grad_value: float32 [768, 384], P('shard')
- grad_depth: float32 [9, 768], P(None, 'shard')
- grad_keyconv: float32 [768, 384], P('shard')
- grad_kernel: float32 [54, 384], P(None, 'shard')
- grad_convout: float32 [768, 384], P('shard')
- grad_output: float32 [768, 768], P('shard')
- grad_gain_attn: float32 [768], P('shard')
- grad_inter: float32 [2, 384, 1536], P(None, None, 'shard')
- grad_outer: float32 [2, 1536, 384], P(None, 'shard')
- grad_gain_ffn: float32 [768], P('shard')
The draws below stay inside these ranges and needn't reach their ends.
Inputs may be any that keep to these rules, and one draw needn't show every extreme that they name: `segment_ids`: segment ids never fall along a sequence; each of the 8 documents of a sequence has 1 to 800 tokens, one exactly 800.
All inputs are finite; a program needn't handle non-finite values.
Results may differ from the reference program's by a relative error of at most 0.015.
Values may be sent and summed in bfloat16 or wider, within the bound.
A program may use at most 192 MiB of HBM per device.

```python
import math
import jax
import jax.numpy as jnp
import numpy as np
from jax import lax

D = 768
HEADS = 6
HS = 64
FF = 3072
KS = 9
GROUPS = 2
LEN = 1024
SEQS = 32
TOKENS = 32768
DOCS = 8
MOST = 800
BLOCK = 512


def draw_cotangent(key, part):
    first_key, second_key = jax.random.split(key, 2)
    row_frac = jnp.arange(TOKENS, dtype=jnp.float32) / max(TOKENS - 1, 1)
    rising = jnp.exp(row_frac * math.log(3.0))[:, None]
    spread = jnp.exp(jax.random.uniform(second_key, (TOKENS, 1), jnp.float32, 0.0, math.log(4.0)))
    base_draw = jnp.clip(jax.random.normal(first_key, (TOKENS, D), jnp.float32), -4.0, 4.0)
    return (base_draw * rising * spread * 0.5).astype(jnp.bfloat16)


def shard_levels(stream_key, dims, pieces, least, high):
    factor_of = 1.0
    for dim, parts in pieces:
        steps = jax.random.uniform(jax.random.fold_in(jax.random.fold_in(stream_key, 6), dim), (parts,), jnp.float32, least / len(pieces), high / len(pieces))
        factor_of = factor_of * jnp.repeat(jnp.exp(steps), dims[dim] // parts).reshape((-1,) + (1,) * (len(dims) - 1 - dim))
    return factor_of


def length_profile(amount, total, most, skew):
    weights = [(1 << 20) // math.isqrt(grade ** skew) + 1 for grade in range(2, amount + 1)]
    rest, holding = total - most - (amount - 1), [1] * (amount - 1)
    while rest > 0:
        candidates = [i for i in range(amount - 1) if holding[i] < most]
        pool, left = sum([weights[i] for i in candidates]), rest
        for i in candidates:
            extra = min(most - holding[i], max(1, left * weights[i] // pool), rest)
            holding[i] = holding[i] + extra
            rest = rest - extra
    return np.array([most] + holding)


def uneven_parts(own_key, count, total, limit, slope):
    if count == 2:
        one = jax.random.randint(own_key, (), max(1, total - limit), min(limit, total - 1) + 1)
        return jnp.stack([one, total - one])
    tallies = jnp.asarray(length_profile(count, total, limit, slope), jnp.int32)
    pairs = (count - 1) // 2
    giver, taker = tallies[1:1 + 2 * pairs:2], tallies[2:2 + 2 * pairs:2]
    room = jnp.minimum(giver - 1, limit - taker)
    moved = jax.random.randint(jax.random.fold_in(own_key, 1), (pairs,), 0, 1 << 20) % (room + 1)
    tallies = tallies.at[1:1 + 2 * pairs:2].set(giver - moved).at[2:2 + 2 * pairs:2].set(taker + moved)
    return tallies[jax.random.permutation(jax.random.fold_in(own_key, 2), count)]


def bell_draw(key, dims, scale, reach, pieces=(), kind=jnp.bfloat16):
    entries = scale * jax.random.normal(key, dims, jnp.float32)
    if pieces:
        entries = entries * shard_levels(key, dims, pieces, -0.22, 0.18)
    return jnp.clip(entries, -reach, reach).astype(kind)


def setup_inputs(seed: int = 0) -> dict:
    streams_of = jax.random.split(jax.random.key(seed), 16)
    hidden = bell_draw(streams_of[0], (TOKENS, D), 1.0, 6.0, ((0, 32),))
    segment_ids = jax.vmap(lambda own: jnp.searchsorted(jnp.cumsum(uneven_parts(own, DOCS, LEN, MOST, 1)), jnp.arange(LEN), side="right"))(jax.random.split(streams_of[1], SEQS)).reshape((SEQS, LEN)).astype(jnp.int32)
    cotangent = draw_cotangent(jax.random.fold_in(streams_of[15], 71), 0)
    w_query = bell_draw(streams_of[3], (D, HEADS * HS), D ** -0.5, 0.21875, ((0, 8),))
    w_key = bell_draw(streams_of[4], (D, HEADS * HS), D ** -0.5, 0.21875, ((0, 8),))
    w_value = bell_draw(streams_of[5], (D, HEADS * HS), D ** -0.5, 0.21875, ((0, 8),))
    w_depth = bell_draw(streams_of[6], (KS, D), KS ** -0.5, 2.0, ((1, 8),))
    w_keyconv = bell_draw(streams_of[7], (D, HEADS * HS), D ** -0.5, 0.21875, ((0, 8),))
    w_kernel = bell_draw(streams_of[8], (HEADS * KS, HEADS * HS), (HEADS * HS) ** -0.5, 0.3125, ((1, 8),))
    w_convout = bell_draw(streams_of[9], (D, HEADS * HS), D ** -0.5, 0.21875, ((0, 8),))
    w_output = bell_draw(streams_of[10], (D, D), (D // 16) ** -0.5, 0.875, ((0, 8),))
    gain_attn = jnp.clip(1.0 + 0.1 * jax.random.normal(streams_of[11], (D,), jnp.float32), 0.5, 1.5).astype(jnp.bfloat16)
    w_inter = bell_draw(streams_of[12], (GROUPS, D // GROUPS, FF // GROUPS), (D // GROUPS) ** -0.5, 0.3125, ((2, 8),))
    w_outer = bell_draw(streams_of[13], (GROUPS, FF // GROUPS, D // GROUPS), (FF // GROUPS) ** -0.5, 0.15625, ((1, 8),))
    gain_ffn = jnp.clip(1.0 + 0.1 * jax.random.normal(streams_of[14], (D,), jnp.float32), 0.5, 1.5).astype(jnp.bfloat16)
    return {"hidden": hidden, "segment_ids": segment_ids, "cotangent": cotangent, "w_query": w_query, "w_key": w_key, "w_value": w_value, "w_depth": w_depth, "w_keyconv": w_keyconv, "w_kernel": w_kernel, "w_convout": w_convout, "w_output": w_output, "gain_attn": gain_attn, "w_inter": w_inter, "w_outer": w_outer, "gain_ffn": gain_ffn}


@jax.custom_vjp
def low(v):
    return lax.optimization_barrier(v.astype(jnp.bfloat16)).astype(jnp.float32)

@jax.custom_vjp
def low_back(v):
    return v

def low_keep(v):
    return (low(v), None)

def low_pass(kept, grad):
    return (grad,)

def back_keep(v):
    return (v, None)

def back_low(kept, grad):
    return (low(grad),)
low.defvjp(low_keep, low_pass)
low_back.defvjp(back_keep, back_low)
highest = lax.Precision.HIGHEST
epsilon = 1e-05
masked_value = -1000000000.0
inv_root_two = 0.7071067811865476

def narrow(value):
    return low(low_back(value))

def matmul(left, right):
    return jnp.dot(left, right, precision=highest)

def shifted(value, segment, offset):
    half_taps = (KS - 1) // 2
    length = value.shape[0]
    padded = jnp.pad(value, ((half_taps, half_taps), (0, 0)))
    seg_padded = jnp.pad(segment, (half_taps, half_taps), constant_values=-1)
    moved_rows = lax.slice_in_dim(padded, half_taps + offset, half_taps + offset + length, axis=0)
    moved_segs = lax.slice_in_dim(seg_padded, half_taps + offset, half_taps + offset + length, axis=0)
    same_doc = moved_segs == segment
    return jnp.where(same_doc[:, None], moved_rows, jnp.zeros_like(moved_rows))

def normalize(value, gain_row):
    centered = value - lax.optimization_barrier(jnp.mean(value, axis=1, keepdims=True))
    row_scale = lax.rsqrt(lax.optimization_barrier(jnp.mean(centered * centered, axis=1, keepdims=True)) + epsilon)
    return centered * row_scale * gain_row[None, :]

def gelu_exact(value):
    return 0.5 * value * (1.0 + lax.erf(value * inv_root_two))

def attend(query_block, seg_block, keys_heads, values_heads, segment):
    raw_scores = jnp.einsum('qhd,khd->hqk', query_block, keys_heads, precision=highest) * HS ** (-0.5)
    scores = low_back(raw_scores)
    live = (seg_block[:, None] == segment[None, :])[None, :, :]
    scores = jnp.where(live, scores, masked_value)
    row_top = lax.optimization_barrier(jnp.max(scores, axis=2, keepdims=True))
    weights = jnp.exp(scores - row_top)
    probs = weights / lax.optimization_barrier(jnp.sum(weights, axis=2, keepdims=True))
    return jnp.einsum('hqk,khd->qhd', low(probs), values_heads, precision=highest)

def layer_math(seq_rows, segment, w_query, w_key, w_value, w_depth, w_keyconv, w_kernel, w_convout, w_output, gain_attn, w_inter, w_outer, gain_ffn):
    att_width = HEADS * HS
    half_taps = (KS - 1) // 2
    queries = narrow(matmul(seq_rows, w_query))
    keys_all = narrow(matmul(seq_rows, w_key))
    values_all = narrow(matmul(seq_rows, w_value))
    depth_mix = narrow(sum((w_depth[tap_index][None, :] * shifted(seq_rows, segment, tap_index - half_taps) for tap_index in range(KS))))
    keyconv = low_back(matmul(depth_mix, w_keyconv))
    mixed_key = narrow(keyconv * queries)
    logits = low_back(matmul(mixed_key, w_kernel.T)).reshape(LEN, HEADS, KS)
    row_top = lax.optimization_barrier(jnp.max(logits, axis=2, keepdims=True))
    weights = jnp.exp(logits - row_top)
    tap_weights = weights / lax.optimization_barrier(jnp.sum(weights, axis=2, keepdims=True))
    conv_values = low_back(matmul(seq_rows, w_convout))
    conv_mix = sum((tap_weights[:, :, tap_index, None] * shifted(conv_values, segment, tap_index - half_taps).reshape(LEN, HEADS, HS) for tap_index in range(KS))).reshape(LEN, att_width)
    query_blocks = queries.reshape(LEN // BLOCK, BLOCK, HEADS, HS)
    seg_blocks = segment.reshape(LEN // BLOCK, BLOCK)
    keys_heads = keys_all.reshape(LEN, HEADS, HS)
    values_heads = values_all.reshape(LEN, HEADS, HS)

    def block_math(block_item):
        return attend(block_item[0], block_item[1], keys_heads, values_heads, segment)
    attended = lax.map(jax.checkpoint(block_math), (query_blocks, seg_blocks)).reshape(LEN, att_width)
    context = narrow(jnp.concatenate([attended, conv_mix], axis=1))
    first_sum = low_back(matmul(context, w_output)) + seq_rows
    normed = normalize(first_sum, gain_attn)
    normed_low = low(normed).reshape(LEN, GROUPS, D // GROUPS)
    inner = low_back(jnp.einsum('lgd,gdf->lgf', normed_low, w_inter, precision=highest))
    activated = low(gelu_exact(inner))
    second_sum = low_back(jnp.einsum('lgf,gfd->lgd', activated, w_outer, precision=highest).reshape(LEN, D)) + normed
    return normalize(second_sum, gain_ffn)

def reference(hidden, segment_ids, cotangent, w_query, w_key, w_value, w_depth, w_keyconv, w_kernel, w_convout, w_output, gain_attn, w_inter, w_outer, gain_ffn):
    params = tuple((weight.astype(jnp.float32) for weight in (w_query, w_key, w_value, w_depth, w_keyconv, w_kernel, w_convout, w_output, gain_attn, w_inter, w_outer, gain_ffn)))
    seq_rows = hidden.reshape(SEQS, LEN, D)
    seq_grads = cotangent.reshape(SEQS, LEN, D)

    def one_sequence(totals, seq_item):
        rows_in, segment, grad_in = seq_item

        def forward(rows_float, *weights_float):
            return layer_math(rows_float, segment, *weights_float)
        result, pull = jax.vjp(forward, rows_in.astype(jnp.float32), *params)
        pulled = pull(grad_in.astype(jnp.float32))
        totals = tuple((carried + fresh for carried, fresh in zip(totals, pulled[1:])))
        return (totals, (result.astype(jnp.bfloat16), pulled[0]))
    start = tuple((jnp.zeros(weight.shape, jnp.float32) for weight in params))
    totals, (outputs, input_grads) = lax.scan(one_sequence, start, (seq_rows, segment_ids, seq_grads))
    return (outputs.reshape(TOKENS, D), input_grads.reshape(TOKENS, D), totals[0], totals[1], totals[2], totals[3], totals[4], totals[5], totals[6], totals[7], totals[8], totals[9], totals[10], totals[11])
```

```python
import functools
import math

import jax
import jax.numpy as jnp
from jax import lax
from jax.experimental import pallas as pl
from jax.experimental.pallas import tpu as pltpu
from jax.sharding import PartitionSpec as P

f32 = jnp.float32
bf16 = jnp.bfloat16
EPS = 1e-05
FAR = 1e9
WIDTH = 384
LANES = 128
SLOT = 8
BLK = 256
AUG = 16
INV_SQRT2 = 0.7071067811865476
INV_SQRT2PI = 0.3989422804014327


def dg(left, right, cl, cr):
    return lax.dot_general(
        left, right, (((cl,), (cr,)), ((), ())), preferred_element_type=f32
    )


def up(value, unit):
    return -(-value // unit) * unit


class Plan:
    def __init__(self, shards, model, att, ff_rows, groups):
        self.shards = shards
        self.rows_in = model // shards
        self.rows_ff = ff_rows // shards
        self.rows_small = up(att // shards, 16)
        self.n_small = att // shards
        self.offset = {}
        self.count = {}
        at = 0
        for name, n in (
            [(k, self.rows_in) for k in ("query", "key", "value", "keyconv", "convout")]
            + [("small", self.rows_small)]
            + [("out0", self.rows_in), ("out1", self.rows_in)]
            + [("inter%d" % g, self.rows_ff) for g in range(groups)]
            + [("outer%d" % g, self.rows_ff) for g in range(groups)]
        ):
            self.offset[name] = at
            self.count[name] = n
            at += n
        self.rows = at


FRONT = ("query", "key", "value", "keyconv", "convout", "small")


def mega(
    plan, heads, taps, length, model,
    hid, cot, segr, gath,
    out_ref, hg, grads, probs_hbm,
    wts, smalls, segb, cmf, qaT, kaT, vaT, qs, cvf, tw, depth_low, kc, mixed,
    ctx, attT, linv, prob, expand, gn, dout, stage, dsem,
):
    half = (taps - 1) // 2
    att = heads * (WIDTH // heads)
    hs = att // heads
    groups = model // WIDTH
    cols_m = model // LANES
    cols_a = att // LANES
    nblk = length // BLK
    PADR = 8
    span = taps * LANES

    names = list(FRONT) + [n for n in plan.offset if n not in FRONT]
    wcopies = {}
    for i, name in enumerate(names):
        dst = smalls if name == "small" else wts[name]
        wcopies[name] = pltpu.make_async_copy(
            gath.at[:, pl.ds(plan.offset[name], plan.count[name]), :], dst, dsem.at[i]
        )
        wcopies[name].start()

    part = plan.shards // 2
    nff = plan.shards * plan.rows_ff

    def weight(name, k=None):
        ref = wts[name]
        value = ref[...] if k is None else ref[k * part:(k + 1) * part]
        return value.reshape(value.shape[0] * value.shape[1], WIDTH)

    def rows_of(b):
        return pl.ds(pl.multiple_of(b * BLK, BLK), BLK)

    def blocks(body, n=nblk):
        def step(b, carry):
            body(b)
            return carry
        lax.fori_loop(0, n, step, 0)

    segf = segr[...].astype(f32)
    wide = jnp.broadcast_to(segf, (LANES, length)).T
    edge = jnp.full((PADR, LANES), -1.0, f32)
    segb[0:PADR, :] = edge
    segb[PADR + length:, :] = edge
    segb[pl.ds(PADR, length), :] = wide

    def pad_edges(ref):
        for c in range(ref.shape[0]):
            ref[c, 0:PADR, :] = jnp.zeros((PADR, LANES), f32)
            ref[c, PADR + length:, :] = jnp.zeros((PADR, LANES), f32)
    pad_edges(cvf)

    def masks(b):
        base = pl.multiple_of(b * BLK, BLK)
        own = segb[pl.ds(base + PADR, BLK), :]
        slot = lax.broadcasted_iota(jnp.int32, (BLK, LANES), 1) // SLOT
        acc = jnp.zeros((BLK, LANES), f32)
        for t in range(taps):
            same = segb[pl.ds(base + PADR + t - half, BLK), :] == own
            acc = jnp.where((slot == t) & same, 1.0, acc)
        cmf[rows_of(b), :] = acc
    blocks(masks)

    iota_r = lax.broadcasted_iota(jnp.int32, (2 * LANES, LANES), 0) % LANES
    iota_c = lax.broadcasted_iota(jnp.int32, (2 * LANES, LANES), 1)
    for c in range(cols_a):
        for t in range(taps):
            want = t * SLOT + (c * LANES + iota_c) // hs
            expand[:, c * span + t * LANES:c * span + (t + 1) * LANES] = jnp.where(
                iota_r == want, 1.0, 0.0
            ).astype(bf16)

    lane16 = lax.broadcasted_iota(jnp.int32, (AUG, length), 0).astype(f32)
    seg16 = jnp.broadcast_to(segf, (AUG, length))
    q_extra = jnp.where(lane16 == seg16, 0.0, jnp.where(lane16 < 8.0, -FAR, 0.0)).astype(bf16)
    k_extra = jnp.where(lane16 == seg16, 1.0, 0.0).astype(bf16)
    v_extra = jnp.where(lane16 < 3.0, 1.0, 0.0).astype(bf16)
    for h in range(heads):
        qaT[h, hs:, :] = q_extra
        kaT[h, hs:, :] = k_extra
        vaT[h, hs:, :] = v_extra

    wcopies["small"].wait()
    ns = plan.n_small
    wkT = jnp.concatenate(
        [smalls[s, :, 0:LANES].astype(f32)[0:ns] for s in range(plan.shards)], axis=0
    ).astype(bf16)
    per_feature = jnp.concatenate(
        [
            smalls[s, :, (1 + j) * LANES:(2 + j) * LANES].astype(f32)[0:ns]
            for s in range(plan.shards)
            for j in range(2)
        ],
        axis=0,
    )
    gn[0:AUG, :] = per_feature.T[0:AUG, :]
    gain_a = gn[taps:taps + 1, :]
    gain_f = gn[taps + 1:taps + 2, :]

    CH = 64

    def depth_scope(xf):
        pad_edges(xf)

        def fill(b):
            base = pl.multiple_of(b * BLK, BLK)
            for c in range(cols_m):
                xf[c, pl.ds(base + PADR, BLK), :] = hid[rows_of(b), c * LANES:(c + 1) * LANES].astype(f32)
        blocks(fill)

        def depth_chunk(b, carry):
            base = pl.multiple_of(b * CH, CH)
            own = segb[pl.ds(base + PADR, CH), :]
            accs = [jnp.zeros((CH, LANES), f32) for _ in range(cols_m)]
            for t in range(taps):
                at = base + PADR + t - half
                same = segb[pl.ds(at, CH), :] == own
                for c in range(cols_m):
                    tap = gn[t:t + 1, c * LANES:(c + 1) * LANES]
                    accs[c] = accs[c] + jnp.where(same, xf[c, pl.ds(at, CH), :], 0.0) * tap
            for c in range(cols_m):
                depth_low[pl.ds(base, CH), c * LANES:(c + 1) * LANES] = accs[c].astype(bf16)
            return carry
        lax.fori_loop(0, length // CH, depth_chunk, 0)
    pl.run_scoped(depth_scope, pltpu.VMEM((cols_m, length + 2 * PADR, LANES), f32))

    for name in ("query", "key", "value", "convout", "keyconv"):
        wcopies[name].wait()

    def project(b):
        r = rows_of(b)
        rows = hid[r, :]
        q = dg(rows, weight("query"), 1, 0).astype(bf16)
        qs[r, :] = q
        qT = (q.astype(f32) * (hs ** -0.5)).astype(bf16).T
        kT = dg(rows, weight("key"), 1, 0).astype(bf16).T
        vT = dg(rows, weight("value"), 1, 0).astype(bf16).T
        for h in range(heads):
            qaT[h, 0:hs, r] = qT[h * hs:(h + 1) * hs]
            kaT[h, 0:hs, r] = kT[h * hs:(h + 1) * hs]
            vaT[h, 0:hs, r] = vT[h * hs:(h + 1) * hs]
        cv = dg(rows, weight("convout"), 1, 0)
        for c in range(cols_a):
            cvf[c, pl.ds(pl.multiple_of(b * BLK, BLK) + PADR, BLK), :] = cv[:, c * LANES:(c + 1) * LANES]
        keyconv = dg(depth_low[r, :], weight("keyconv"), 1, 0)
        kc[r, :] = keyconv
        mk = (keyconv * q.astype(f32)).astype(bf16)
        mixed[r, :] = mk
        logits = dg(mk, wkT, 1, 0)
        lane = lax.broadcasted_iota(jnp.int32, logits.shape, 1)
        logits = jnp.where(lane < taps * SLOT, logits, -1e30)
        top = logits
        for s in (64, 32, 16, 8):
            top = jnp.maximum(top, pltpu.roll(top, b * 0 + s, 1))
        e = jnp.exp(logits - top)
        total = e
        for s in (64, 32, 16, 8):
            total = total + pltpu.roll(total, b * 0 + s, 1)
        tw[r, :] = e / total
    blocks(project)

    def split(value):
        high = value.astype(bf16)
        low = (value - high.astype(f32)).astype(bf16)
        return jnp.concatenate([high, low], axis=1)

    CV = 128

    def conv_chunk(b, carry):
        base = pl.multiple_of(b * CV, CV)
        r = pl.ds(base, CV)
        pair = split(tw[r, :] * cmf[r, :])
        for c in range(cols_a):
            big = dg(pair, expand[:, c * span:(c + 1) * span], 1, 0)
            acc = jnp.zeros((CV, LANES), f32)
            for t in range(taps):
                acc = acc + big[:, t * LANES:(t + 1) * LANES] * cvf[c, pl.ds(base + PADR + t - half, CV), :]
            ctx[r, att + c * LANES:att + (c + 1) * LANES] = acc.astype(bf16)
        return carry
    lax.fori_loop(0, length // CV, conv_chunk, 0)

    def p_out(h):
        return pltpu.make_async_copy(prob.at[h % 2], probs_hbm.at[h], dsem.at[len(names) + h % 2])

    for h in range(heads):
        if 2 <= h:
            p_out(h - 2).wait()

        def fwd(b, h=h):
            r = rows_of(b)
            s = dg(qaT[h, :, r], kaT[h], 0, 0)
            top = jnp.max(s, axis=1, keepdims=True)
            e = jnp.exp(s - top).astype(bf16)
            prob[h % 2, r, :] = e
            o = dg(vaT[h], e, 1, 1)
            inv = 1.0 / o[hs:hs + 1, :]
            linv[h:h + 1, r] = inv
            attT[h * hs:(h + 1) * hs, r] = o[0:hs, :] * inv
        blocks(fwd)
        if h < heads - 2:
            p_out(h).start()

    def to_ctx(b):
        r = rows_of(b)
        ctx[r, 0:att] = attT[:, r].astype(bf16).T
    blocks(to_ctx)

    for name in names:
        if name not in FRONT:
            wcopies[name].wait()

    def norm_back(grad, unit, scale, gain):
        e = grad * gain
        inside = e - jnp.mean(e, axis=1, keepdims=True) - unit * jnp.mean(e * unit, axis=1, keepdims=True)
        return scale * inside

    send = {}

    def outgoing(name, slot):
        n = plan.count[name]
        return pltpu.make_async_copy(
            stage.at[slot, pl.ds(0, plan.shards * n)].reshape(plan.shards, n, WIDTH),
            grads.at[:, pl.ds(plan.offset[name], n), :],
            dsem.at[len(names) + 2 + slot],
        )

    def drain(slot):
        if slot in send:
            outgoing(send.pop(slot), slot).wait()

    def ship(name, value, slot):
        drain(slot)
        stage[slot, 0:plan.shards * plan.count[name], :] = value.astype(bf16)
        outgoing(name, slot).start()
        send[slot] = name

    def mid_scope(act, dinner, nl, db, slope):
        gn[AUG:AUG + 2 * SLOT, :] = jnp.zeros((2 * SLOT, model), f32)

        def mid(b):
            r = rows_of(b)
            c = ctx[r, :]
            first = jnp.concatenate(
                [dg(c, weight("out%d" % j), 1, 0) for j in range(groups)], axis=1
            ) + hid[r, :].astype(f32)
            cen = first - jnp.mean(first, axis=1, keepdims=True)
            s1 = lax.rsqrt(jnp.mean(cen * cen, axis=1, keepdims=True) + EPS)
            unit1 = cen * s1
            normed = unit1 * gain_a
            low = normed.astype(bf16)
            nl[r, :] = low
            ffs = []
            for g in range(groups):
                total = jnp.zeros((BLK, WIDTH), f32)
                for k in range(plan.shards // part):
                    inner = dg(low[:, g * WIDTH:(g + 1) * WIDTH], weight("inter%d" % g, k), 1, 1)
                    at = g * nff + k * inner.shape[1]
                    phi = 0.5 + 0.5 * lax.erf(inner * INV_SQRT2)
                    a = (inner * phi).astype(bf16)
                    act[r, at:at + inner.shape[1]] = a
                    slope[:, at:at + inner.shape[1]] = (
                        phi + inner * jnp.exp(inner * inner * -0.5) * INV_SQRT2PI
                    ).astype(bf16)
                    total = total + dg(a, weight("outer%d" % g, k), 1, 0)
                ffs.append(total)
            second = jnp.concatenate(ffs, axis=1) + normed
            cen2 = second - jnp.mean(second, axis=1, keepdims=True)
            s2 = lax.rsqrt(jnp.mean(cen2 * cen2, axis=1, keepdims=True) + EPS)
            unit2 = cen2 * s2
            out_ref[r, :] = (unit2 * gain_f).astype(bf16)
            dy = cot[r, :].astype(f32)
            gn[AUG:AUG + SLOT, :] += jnp.sum((dy * unit2).reshape(BLK // SLOT, SLOT, model), axis=0)
            dsec = norm_back(dy, unit2, s2, gain_f)
            dlow = dsec.astype(bf16)
            db[r, :] = dlow
            backs = []
            for g in range(groups):
                total = jnp.zeros((BLK, WIDTH), f32)
                for k in range(plan.shards // part):
                    da = dg(dlow[:, g * WIDTH:(g + 1) * WIDTH], weight("outer%d" % g, k), 1, 1)
                    at = g * nff + k * da.shape[1]
                    di = (da * slope[:, at:at + da.shape[1]].astype(f32)).astype(bf16)
                    dinner[r, at:at + da.shape[1]] = di
                    total = total + dg(di, weight("inter%d" % g, k), 1, 0)
                backs.append(total)
            dn = dsec + jnp.concatenate(backs, axis=1)
            gn[AUG + SLOT:AUG + 2 * SLOT, :] += jnp.sum((dn * unit1).reshape(BLK // SLOT, SLOT, model), axis=0)
            dfirst = norm_back(dn, unit1, s1, gain_a)
            hg[r, :] = dfirst
            do = dfirst.astype(bf16)
            dout[r, :] = do
        blocks(mid)

        for g in range(groups):
            cols = slice(g * WIDTH, (g + 1) * WIDTH)
            for slot, (name, left, right) in enumerate((("outer", act, db), ("inter", dinner, nl))):
                drain(slot)
                for k in range(4):
                    n = nff // 4
                    at = g * nff + k * n
                    stage[slot, k * n:(k + 1) * n, :] = dg(left[:, at:at + n], right[:, cols], 0, 0).astype(bf16)
                outgoing("%s%d" % (name, g), slot).start()
                send[slot] = "%s%d" % (name, g)

    ff = 2 * plan.rows_ff * plan.shards
    pl.run_scoped(
        mid_scope,
        pltpu.VMEM((length, ff), bf16),
        pltpu.VMEM((length, ff), bf16),
        pltpu.VMEM((length, model), bf16),
        pltpu.VMEM((length, model), bf16),
        pltpu.VMEM((BLK, ff), bf16),
    )

    def back_scope(xf, doaT, dS, dall, dkc, dlog, dcv, prod, gd):
        for j in range(groups):
            ship("out%d" % j, dg(ctx[...], dout[:, j * WIDTH:(j + 1) * WIDTH], 0, 0), j % 2)

        def dctx(b):
            r = rows_of(b)
            d = dout[r, :]
            full = sum(
                dg(d[:, j * WIDTH:(j + 1) * WIDTH], weight("out%d" % j), 1, 1) for j in range(groups)
            ).astype(bf16)
            ctx[r, att:] = full[:, att:]
            dT = full[:, 0:att].T.astype(f32)
            for h in range(heads):
                scaled = (dT[h * hs:(h + 1) * hs] * linv[h:h + 1, r]).astype(bf16)
                doaT[h, 0:hs, r] = scaled
                drop = -jnp.sum(scaled.astype(f32) * attT[h * hs:(h + 1) * hs, r], axis=0, keepdims=True)
                d1 = drop.astype(bf16).astype(f32)
                d2 = (drop - d1).astype(bf16).astype(f32)
                d3 = drop - d1 - d2
                line = lax.broadcasted_iota(jnp.int32, (AUG, BLK), 0)
                extra = jnp.where(line == 0, d1, jnp.where(line == 1, d2, jnp.where(line == 2, d3, 0.0)))
                doaT[h, hs:, r] = extra.astype(bf16)
        blocks(dctx)

        order = [heads - 2, heads - 1] + list(range(heads - 2))

        def p_in(h, slot):
            return pltpu.make_async_copy(probs_hbm.at[h], prob.at[slot], dsem.at[len(names) + slot])

        for i, h in enumerate(order):
            slot = i % 2 if heads % 2 == 0 else (heads - 2 + i) % 2
            if i >= 2:
                p_in(h, slot).wait()

            def bwd(b, h=h, slot=slot):
                r = rows_of(b)
                dp = dg(doaT[h, :, r], vaT[h], 0, 0)
                dS[r, :] = (prob[slot, r, :].astype(f32) * dp).astype(bf16)
            blocks(bwd)
            dqT = dg(kaT[h, 0:hs, :], dS[...], 1, 1) * (hs ** -0.5)
            dkT = dg(qaT[h, 0:hs, :], dS[...], 1, 0)
            dvT = dg(doaT[h, 0:hs, :], prob[slot], 1, 0)
            attT[h * hs:(h + 1) * hs, :] = dqT
            kaT[h, 0:hs, :] = dkT.astype(bf16)
            vaT[h, 0:hs, :] = dvT.astype(bf16)
            if i + 2 < heads:
                p_in(order[i + 2], slot).start()

        pad_edges(xf)
        for c in range(cols_a):
            dcv[c, :, :] = jnp.zeros((length + 2 * PADR, LANES), f32)

        def conv_back(b, carry):
            base = pl.multiple_of(b * CV, CV)
            r = pl.ds(base, CV)
            w = tw[r, :]
            mask = cmf[r, :]
            pair = split(w * mask)
            dt = jnp.zeros((CV, LANES), f32)
            for c in range(cols_a):
                dc = ctx[r, att + c * LANES:att + (c + 1) * LANES].astype(f32)
                big = dg(pair, expand[:, c * span:(c + 1) * span], 1, 0)
                for t in range(taps):
                    at = base + PADR + t - half
                    prod[:, t * LANES:(t + 1) * LANES] = (dc * cvf[c, pl.ds(at, CV), :]).astype(bf16)
                    dcv[c, pl.ds(at, CV), :] += big[:, t * LANES:(t + 1) * LANES] * dc
                dt = dt + dg(prod[...], expand[0:LANES, c * span:(c + 1) * span], 1, 1)
            dt = dt * mask
            total = dt * w
            for s in (64, 32, 16, 8):
                total = total + pltpu.roll(total, b * 0 + s, 1)
            dl = (w * (dt - total)).astype(bf16)
            dlog[r, :] = dl
            dm = dg(dl, wkT, 1, 1).astype(bf16).astype(f32)
            dkc[r, :] = (dm * qs[r, :].astype(f32)).astype(bf16)
            kc[r, :] = dm * kc[r, :]
            return carry
        lax.fori_loop(0, length // CV, conv_back, 0)

        def collect(b):
            r = rows_of(b)
            at = pl.multiple_of(b * BLK, BLK) + PADR
            dall[r, 0:att] = (attT[:, r].T + kc[r, :]).astype(bf16)
            for h in range(heads):
                pass
            kk = jnp.concatenate([kaT[h, 0:hs, r] for h in range(heads)], axis=0)
            vv = jnp.concatenate([vaT[h, 0:hs, r] for h in range(heads)], axis=0)
            dall[r, att:2 * att] = kk.T
            dall[r, 2 * att:3 * att] = vv.T
            for c in range(cols_a):
                dall[r, 3 * att + c * LANES:3 * att + (c + 1) * LANES] = dcv[c, pl.ds(at, BLK), :].astype(bf16)
            dd = dg(dkc[r, :], weight("keyconv"), 1, 1).astype(bf16).astype(f32)
            for c in range(cols_m):
                xf[c, pl.ds(at, BLK), :] = dd[:, c * LANES:(c + 1) * LANES]
            total = hg[r, :]
            for j, name in enumerate(("query", "key", "value", "convout")):
                total = total + dg(dall[r, j * att:(j + 1) * att], weight(name), 1, 1)
            hg[r, :] = total
        blocks(collect)

        ship("keyconv", dg(depth_low[...], dkc[...], 0, 0), 0)
        for j, name in enumerate(("query", "key", "value", "convout")):
            ship(name, dg(hid[...], dall[:, j * att:(j + 1) * att], 0, 0), (j + 1) % 2)

        gk = dg(mixed[...], dlog[...], 0, 0)

        gd[...] = jnp.zeros(gd.shape, f32)

        def depth_back(b, carry):
            base = pl.multiple_of(b * CH, CH)
            own = segb[pl.ds(base + PADR, CH), :]
            r = pl.ds(base, CH)
            sames = [segb[pl.ds(base + PADR + t - half, CH), :] == own for t in range(taps)]
            for c in range(cols_m):
                lanes = slice(c * LANES, (c + 1) * LANES)
                x = hid[r, lanes].astype(f32)
                acc = hg[r, lanes]
                for t in range(taps):
                    back = taps - 1 - t
                    v = jnp.where(sames[t], xf[c, pl.ds(base + PADR + t - half, CH), :], 0.0)
                    acc = acc + v * gn[back:back + 1, lanes]
                    gd[back, :, lanes] += jnp.sum((v * x).reshape(CH // SLOT, SLOT, LANES), axis=0)
                hg[r, lanes] = acc
            return carry
        lax.fori_loop(0, length // CH, depth_back, 0)

        rows = [jnp.sum(gd[t], axis=0, keepdims=True) for t in range(taps)]
        rows.append(jnp.sum(gn[AUG + SLOT:AUG + 2 * SLOT, :], axis=0, keepdims=True))
        rows.append(jnp.sum(gn[AUG:AUG + SLOT, :], axis=0, keepdims=True))
        rows.append(jnp.zeros((LANES - len(rows), model), f32))
        pf = jnp.concatenate(rows, axis=0).T
        slot = 0
        drain(slot)
        nr = plan.rows_small
        for s in range(plan.shards):
            parts = [gk[s * ns:(s + 1) * ns]] + [
                pf[(2 * s + j) * ns:(2 * s + j + 1) * ns] for j in range(2)
            ]
            piece = jnp.concatenate(parts, axis=1)
            if nr > ns:
                piece = jnp.concatenate([piece, jnp.zeros((nr - ns, WIDTH), f32)], axis=0)
            stage[slot, s * nr:(s + 1) * nr, :] = piece.astype(bf16)
        outgoing("small", slot).start()
        send[slot] = "small"
        for slot in sorted(send):
            drain(slot)

    pl.run_scoped(
        back_scope,
        pltpu.VMEM((cols_m, length + 2 * PADR, LANES), f32),
        pltpu.VMEM((heads, hs + AUG, length), bf16),
        pltpu.VMEM((length, length), bf16),
        pltpu.VMEM((length, 4 * att), bf16),
        pltpu.VMEM((length, att), bf16),
        pltpu.VMEM((length, LANES), bf16),
        pltpu.VMEM((cols_a, length + 2 * PADR, LANES), f32),
        pltpu.VMEM((CV, span), bf16),
        pltpu.VMEM((taps, SLOT, model), f32),
    )


def run_mega(plan, heads, taps, hidden, cotangent, segr, gath):
    length, model = hidden.shape
    att = WIDTH
    hs = att // heads
    cols_m, cols_a = model // LANES, att // LANES
    names = [n for n in plan.offset if n != "small"]
    sh = plan.shards
    big = sh * max(plan.rows_in, plan.rows_ff)

    def body(hid, cot, sg, ga, o, h, gr, ph, *rest):
        nw = len(names)
        wts = dict(zip(names, rest[:nw]))
        mega(plan, heads, taps, length, model, hid, cot, sg, ga, o, h, gr, ph, wts, *rest[nw:])

    vm = pl.BlockSpec(memory_space=pltpu.VMEM)
    an = pl.BlockSpec(memory_space=pl.ANY)
    return pl.pallas_call(
        body,
        out_shape=(
            jax.ShapeDtypeStruct((length, model), bf16),
            jax.ShapeDtypeStruct((length, model), f32),
            jax.ShapeDtypeStruct((sh, plan.rows, WIDTH), bf16),
            jax.ShapeDtypeStruct((heads, length, length), bf16),
        ),
        in_specs=[vm, vm, vm, an],
        out_specs=(vm, vm, an, an),
        scratch_shapes=[pltpu.VMEM((sh, plan.count[n], WIDTH), bf16) for n in names]
        + [
            pltpu.VMEM((sh, plan.rows_small, WIDTH), bf16),
            pltpu.VMEM((length + 16, LANES), f32),
            pltpu.VMEM((length, LANES), f32),
            pltpu.VMEM((heads, hs + AUG, length), bf16),
            pltpu.VMEM((heads, hs + AUG, length), bf16),
            pltpu.VMEM((heads, hs + AUG, length), bf16),
            pltpu.VMEM((length, att), bf16),
            pltpu.VMEM((cols_a, length + 16, LANES), f32),
            pltpu.VMEM((length, LANES), f32),
            pltpu.VMEM((length, model), bf16),
            pltpu.VMEM((length, att), f32),
            pltpu.VMEM((length, att), bf16),
            pltpu.VMEM((length, 2 * att), bf16),
            pltpu.VMEM((att, length), f32),
            pltpu.VMEM((SLOT, length), f32),
            pltpu.VMEM((2, length, length), bf16),
            pltpu.VMEM((2 * LANES, cols_a * taps * LANES), bf16),
            pltpu.VMEM((AUG + 2 * SLOT, model), f32),
            pltpu.VMEM((length, model), bf16),
            pltpu.VMEM((2, big, WIDTH), bf16),
            pltpu.SemaphoreType.DMA((len(plan.offset) + 4,)),
        ],
        compiler_params=pltpu.CompilerParams(vmem_limit_bytes=67043328),
    )(hidden, cotangent, segr, gath)


def pack(plan, taps, w_query, w_key, w_value, w_depth, w_keyconv, w_kernel, w_convout, w_output, gain_attn, w_inter, w_outer, gain_ffn):
    ns = plan.n_small
    heads = w_kernel.shape[0] // taps
    wk = w_kernel.reshape(heads, taps, ns).transpose(2, 1, 0)
    wk = jnp.pad(wk, ((0, 0), (0, 0), (0, SLOT - heads))).reshape(ns, taps * SLOT)
    wk = jnp.pad(wk, ((0, 0), (0, LANES - taps * SLOT)))
    pf = jnp.concatenate([w_depth, gain_attn[None], gain_ffn[None]], axis=0).T
    pf = jnp.pad(pf, ((0, 0), (0, LANES - pf.shape[1])))
    small = jnp.concatenate([wk, pf[:ns], pf[ns:]], axis=1)
    small = jnp.pad(small, ((0, plan.rows_small - ns), (0, 0)))
    groups = w_inter.shape[0]
    parts = [w_query, w_key, w_value, w_keyconv, w_convout, small]
    parts += [w_output[:, j * WIDTH:(j + 1) * WIDTH] for j in range(groups)]
    parts += [w_inter[g].T for g in range(groups)]
    parts += [w_outer[g] for g in range(groups)]
    return jnp.concatenate(parts, axis=0)


def unpack(plan, taps, heads, groups, total):
    def part(name):
        return total[plan.offset[name]:plan.offset[name] + plan.count[name]]
    ns = plan.n_small
    small = part("small")[:ns]
    gk = small[:, :taps * SLOT].reshape(ns, taps, SLOT)[:, :, :heads].transpose(2, 1, 0).reshape(heads * taps, ns)
    pf = jnp.concatenate([small[:, LANES:2 * LANES], small[:, 2 * LANES:]], axis=0)
    return (
        part("query"), part("key"), part("value"),
        pf[:, :taps].T,
        part("keyconv"), gk, part("convout"),
        jnp.concatenate([part("out%d" % j) for j in range(groups)], axis=1),
        pf[:, taps],
        jnp.stack([part("inter%d" % g).T for g in range(groups)]),
        jnp.stack([part("outer%d" % g) for g in range(groups)]),
        pf[:, taps + 1],
    )


def local(hidden, segment_ids, cotangent, *weights):
    w_query, w_depth, w_kernel, w_inter, w_outer = weights[0], weights[3], weights[5], weights[9], weights[10]
    shards = lax.axis_size("shard")
    taps = w_depth.shape[0]
    heads = w_kernel.shape[0] // taps
    groups = w_inter.shape[0]
    model = hidden.shape[1]
    plan = Plan(shards, model, w_query.shape[1], w_outer.shape[1] * shards, groups)
    packed = pack(plan, taps, *weights)
    gathered = lax.all_gather(packed, "shard", axis=0)
    output, hidden_grad, grads, _ = run_mega(plan, heads, taps, hidden, cotangent, segment_ids, gathered)
    total = lax.psum_scatter(grads.reshape(shards * plan.rows, WIDTH), "shard", scatter_dimension=0, tiled=True)
    total = lax.psum(total.astype(f32), "rep")
    return (output, hidden_grad, *unpack(plan, taps, heads, groups, total))


def solution(mesh):
    both = P(("rep", "shard"), None)
    rows = P("shard", None)
    cols = P(None, "shard")
    params = (
        rows, rows, rows, cols, rows, cols, rows, rows, P("shard"),
        P(None, None, "shard"), P(None, "shard", None), P("shard"),
    )
    return jax.shard_map(
        local, mesh=mesh, in_specs=(both, both, both) + params, out_specs=(both, both) + params, check_vma=False
    )
```

```python
import functools
import math

import jax
import jax.numpy as jnp
from jax import lax
from jax.experimental import pallas as pl
from jax.experimental.pallas import tpu as pltpu
from jax.sharding import PartitionSpec as P

f32 = jnp.float32
bf16 = jnp.bfloat16
EPS = 1e-05
FAR = 1e9
WIDTH = 384
LANES = 128
SLOT = 8
BLK = 256
AUG = 16
INV_SQRT2 = 0.7071067811865476
INV_SQRT2PI = 0.3989422804014327


def dg(left, right, cl, cr):
    return lax.dot_general(
        left, right, (((cl,), (cr,)), ((), ())), preferred_element_type=f32
    )


def up(value, unit):
    return -(-value // unit) * unit


class Plan:
    def __init__(self, reps, shards, model, att, ff_rows, groups):
        self.reps = reps
        self.shards = shards
        self.rows_in = model // shards
        self.rows_ff = ff_rows // shards
        self.n_small = att // shards
        self.rows_small = up(self.n_small, 16)
        self.offset = {}
        self.count = {}
        self.chunks = []
        self.rows = 0
        front = [(k, self.rows_in) for k in ("query", "key", "value", "keyconv", "convout")]
        front += [("small", self.rows_small)]
        rest = [("out%d" % j, self.rows_in) for j in range(groups)]
        rest += [("inter%d" % g, self.rows_ff) for g in range(groups)]
        rest += [("outer%d" % g, self.rows_ff) for g in range(groups)]
        for part in (front, rest):
            at = self.rows
            for name, n in part:
                self.offset[name] = at
                self.count[name] = n
                at += n
            chunk = up(-(-(at - self.rows) // reps), 16)
            self.chunks.append(chunk)
            self.rows += reps * chunk


FRONT = ("query", "key", "value", "keyconv", "convout", "small")


def mega(
    plan, heads, taps, length, model,
    hid, cot, segr, gath,
    out_ref, hg, grads, probs_hbm,
    wts, smalls, segb, cmf, qaT, kaT, vaT, qs, cvf, tw, depth_low, kc, mixed,
    ctx, attT, linv, prob, expand, gn, dout, stage, dsem,
):
    half = (taps - 1) // 2
    att = heads * (WIDTH // heads)
    hs = att // heads
    groups = model // WIDTH
    cols_m = model // LANES
    cols_a = att // LANES
    nblk = length // BLK
    PADR = 8
    span = taps * LANES

    names = list(FRONT) + [n for n in plan.offset if n not in FRONT]
    wcopies = {}
    for i, name in enumerate(names):
        dst = smalls if name == "small" else wts[name]
        wcopies[name] = pltpu.make_async_copy(
            gath.at[:, pl.ds(plan.offset[name], plan.count[name]), :], dst, dsem.at[i]
        )
        wcopies[name].start()

    part = plan.shards // 2
    nff = plan.shards * plan.rows_ff

    def weight(name, k=None):
        ref = wts[name]
        value = ref[...] if k is None else ref[k * part:(k + 1) * part]
        return value.reshape(value.shape[0] * value.shape[1], WIDTH)

    def rows_of(b):
        return pl.ds(pl.multiple_of(b * BLK, BLK), BLK)

    def blocks(body, n=nblk):
        def step(b, carry):
            body(b)
            return carry
        lax.fori_loop(0, n, step, 0)

    segf = segr[...].astype(f32)
    wide = jnp.broadcast_to(segf, (LANES, length)).T
    edge = jnp.full((PADR, LANES), -1.0, f32)
    segb[0:PADR, :] = edge
    segb[PADR + length:, :] = edge
    segb[pl.ds(PADR, length), :] = wide

    def pad_edges(ref):
        for c in range(ref.shape[0]):
            ref[c, 0:PADR, :] = jnp.zeros((PADR, LANES), f32)
            ref[c, PADR + length:, :] = jnp.zeros((PADR, LANES), f32)
    pad_edges(cvf)

    def masks(b):
        base = pl.multiple_of(b * BLK, BLK)
        own = segb[pl.ds(base + PADR, BLK), :]
        slot = lax.broadcasted_iota(jnp.int32, (BLK, LANES), 1) // SLOT
        acc = jnp.zeros((BLK, LANES), f32)
        for t in range(taps):
            same = segb[pl.ds(base + PADR + t - half, BLK), :] == own
            acc = jnp.where((slot == t) & same, 1.0, acc)
        cmf[rows_of(b), :] = acc
    blocks(masks)

    iota_r = lax.broadcasted_iota(jnp.int32, (2 * LANES, LANES), 0) % LANES
    iota_c = lax.broadcasted_iota(jnp.int32, (2 * LANES, LANES), 1)
    for c in range(cols_a):
        for t in range(taps):
            want = t * SLOT + (c * LANES + iota_c) // hs
            expand[:, c * span + t * LANES:c * span + (t + 1) * LANES] = jnp.where(
                iota_r == want, 1.0, 0.0
            ).astype(bf16)

    lane16 = lax.broadcasted_iota(jnp.int32, (AUG, length), 0).astype(f32)
    seg16 = jnp.broadcast_to(segf, (AUG, length))
    q_extra = jnp.where(lane16 == seg16, 0.0, jnp.where(lane16 < 8.0, -FAR, 0.0)).astype(bf16)
    k_extra = jnp.where(lane16 == seg16, 1.0, 0.0).astype(bf16)
    v_extra = jnp.where(lane16 < 3.0, 1.0, 0.0).astype(bf16)
    for h in range(heads):
        qaT[h, hs:, :] = q_extra
        kaT[h, hs:, :] = k_extra
        vaT[h, hs:, :] = v_extra

    wcopies["small"].wait()
    ns = plan.n_small
    wkT = jnp.concatenate(
        [smalls[s, :, 0:LANES].astype(f32)[0:ns] for s in range(plan.shards)], axis=0
    ).astype(bf16)
    per_feature = jnp.concatenate(
        [
            smalls[s, :, (1 + j) * LANES:(2 + j) * LANES].astype(f32)[0:ns]
            for s in range(plan.shards)
            for j in range(2)
        ],
        axis=0,
    )
    gn[0:AUG, :] = per_feature.T[0:AUG, :]
    gain_a = gn[taps:taps + 1, :]
    gain_f = gn[taps + 1:taps + 2, :]

    CH = 64

    def depth_scope(xf):
        pad_edges(xf)

        def fill(b):
            base = pl.multiple_of(b * BLK, BLK)
            for c in range(cols_m):
                xf[c, pl.ds(base + PADR, BLK), :] = hid[rows_of(b), c * LANES:(c + 1) * LANES].astype(f32)
        blocks(fill)

        def depth_chunk(b, carry):
            base = pl.multiple_of(b * CH, CH)
            own = segb[pl.ds(base + PADR, CH), :]
            accs = [jnp.zeros((CH, LANES), f32) for _ in range(cols_m)]
            for t in range(taps):
                at = base + PADR + t - half
                same = segb[pl.ds(at, CH), :] == own
                for c in range(cols_m):
                    tap = gn[t:t + 1, c * LANES:(c + 1) * LANES]
                    accs[c] = accs[c] + jnp.where(same, xf[c, pl.ds(at, CH), :], 0.0) * tap
            for c in range(cols_m):
                depth_low[pl.ds(base, CH), c * LANES:(c + 1) * LANES] = accs[c].astype(bf16)
            return carry
        lax.fori_loop(0, length // CH, depth_chunk, 0)
    pl.run_scoped(depth_scope, pltpu.VMEM((cols_m, length + 2 * PADR, LANES), f32))

    for name in ("query", "key", "value", "convout", "keyconv"):
        wcopies[name].wait()

    def project(b):
        r = rows_of(b)
        rows = hid[r, :]
        q = dg(rows, weight("query"), 1, 0).astype(bf16)
        qs[r, :] = q
        qT = (q.astype(f32) * (hs ** -0.5)).astype(bf16).T
        kT = dg(rows, weight("key"), 1, 0).astype(bf16).T
        vT = dg(rows, weight("value"), 1, 0).astype(bf16).T
        for h in range(heads):
            qaT[h, 0:hs, r] = qT[h * hs:(h + 1) * hs]
            kaT[h, 0:hs, r] = kT[h * hs:(h + 1) * hs]
            vaT[h, 0:hs, r] = vT[h * hs:(h + 1) * hs]
        cv = dg(rows, weight("convout"), 1, 0)
        for c in range(cols_a):
            cvf[c, pl.ds(pl.multiple_of(b * BLK, BLK) + PADR, BLK), :] = cv[:, c * LANES:(c + 1) * LANES]
        keyconv = dg(depth_low[r, :], weight("keyconv"), 1, 0)
        kc[r, :] = keyconv
        mk = (keyconv * q.astype(f32)).astype(bf16)
        mixed[r, :] = mk
        logits = dg(mk, wkT, 1, 0)
        lane = lax.broadcasted_iota(jnp.int32, logits.shape, 1)
        logits = jnp.where(lane < taps * SLOT, logits, -1e30)
        top = logits
        for s in (64, 32, 16, 8):
            top = jnp.maximum(top, pltpu.roll(top, b * 0 + s, 1))
        e = jnp.exp(logits - top)
        total = e
        for s in (64, 32, 16, 8):
            total = total + pltpu.roll(total, b * 0 + s, 1)
        tw[r, :] = e / total
    blocks(project)

    def split(value):
        high = value.astype(bf16)
        low = (value - high.astype(f32)).astype(bf16)
        return jnp.concatenate([high, low], axis=1)

    CV = 128

    def conv_chunk(b, carry):
        base = pl.multiple_of(b * CV, CV)
        r = pl.ds(base, CV)
        pair = split(tw[r, :] * cmf[r, :])
        for c in range(cols_a):
            big = dg(pair, expand[:, c * span:(c + 1) * span], 1, 0)
            acc = jnp.zeros((CV, LANES), f32)
            for t in range(taps):
                acc = acc + big[:, t * LANES:(t + 1) * LANES] * cvf[c, pl.ds(base + PADR + t - half, CV), :]
            ctx[r, att + c * LANES:att + (c + 1) * LANES] = acc.astype(bf16)
        return carry
    lax.fori_loop(0, length // CV, conv_chunk, 0)

    def p_out(h):
        return pltpu.make_async_copy(prob.at[h % 2], probs_hbm.at[h], dsem.at[len(names) + h % 2])

    for h in range(heads):
        if 2 <= h:
            p_out(h - 2).wait()

        def fwd(b, h=h):
            r = rows_of(b)
            s = dg(qaT[h, :, r], kaT[h], 0, 0)
            top = jnp.max(s, axis=1, keepdims=True)
            e = jnp.exp(s - top).astype(bf16)
            prob[h % 2, r, :] = e
            o = dg(vaT[h], e, 1, 1)
            inv = 1.0 / o[hs:hs + 1, :]
            linv[h:h + 1, r] = inv
            attT[h * hs:(h + 1) * hs, r] = o[0:hs, :] * inv
        blocks(fwd)
        if h < heads - 2:
            p_out(h).start()

    def to_ctx(b):
        r = rows_of(b)
        ctx[r, 0:att] = attT[:, r].astype(bf16).T
    blocks(to_ctx)

    for name in names:
        if name not in FRONT:
            wcopies[name].wait()

    def norm_back(grad, unit, scale, gain):
        e = grad * gain
        inside = e - jnp.mean(e, axis=1, keepdims=True) - unit * jnp.mean(e * unit, axis=1, keepdims=True)
        return scale * inside

    send = {}

    def outgoing(name, slot):
        n = plan.count[name]
        return pltpu.make_async_copy(
            stage.at[slot, pl.ds(0, plan.shards * n)].reshape(plan.shards, n, WIDTH),
            grads.at[:, pl.ds(plan.offset[name], n), :],
            dsem.at[len(names) + 2 + slot],
        )

    def drain(slot):
        if slot in send:
            outgoing(send.pop(slot), slot).wait()

    def ship(name, value, slot):
        drain(slot)
        stage[slot, 0:plan.shards * plan.count[name], :] = value.astype(bf16)
        outgoing(name, slot).start()
        send[slot] = name

    def mid_scope(act, dinner, nl, db, slope):
        gn[AUG:AUG + 2 * SLOT, :] = jnp.zeros((2 * SLOT, model), f32)

        def mid(b):
            r = rows_of(b)
            c = ctx[r, :]
            first = jnp.concatenate(
                [dg(c, weight("out%d" % j), 1, 0) for j in range(groups)], axis=1
            ) + hid[r, :].astype(f32)
            cen = first - jnp.mean(first, axis=1, keepdims=True)
            s1 = lax.rsqrt(jnp.mean(cen * cen, axis=1, keepdims=True) + EPS)
            unit1 = cen * s1
            normed = unit1 * gain_a
            low = normed.astype(bf16)
            nl[r, :] = low
            ffs = []
            for g in range(groups):
                total = jnp.zeros((BLK, WIDTH), f32)
                for k in range(plan.shards // part):
                    inner = dg(low[:, g * WIDTH:(g + 1) * WIDTH], weight("inter%d" % g, k), 1, 1)
                    at = g * nff + k * inner.shape[1]
                    phi = 0.5 + 0.5 * lax.erf(inner * INV_SQRT2)
                    a = (inner * phi).astype(bf16)
                    act[r, at:at + inner.shape[1]] = a
                    slope[:, at:at + inner.shape[1]] = (
                        phi + inner * jnp.exp(inner * inner * -0.5) * INV_SQRT2PI
                    ).astype(bf16)
                    total = total + dg(a, weight("outer%d" % g, k), 1, 0)
                ffs.append(total)
            second = jnp.concatenate(ffs, axis=1) + normed
            cen2 = second - jnp.mean(second, axis=1, keepdims=True)
            s2 = lax.rsqrt(jnp.mean(cen2 * cen2, axis=1, keepdims=True) + EPS)
            unit2 = cen2 * s2
            out_ref[r, :] = (unit2 * gain_f).astype(bf16)
            dy = cot[r, :].astype(f32)
            gn[AUG:AUG + SLOT, :] += jnp.sum((dy * unit2).reshape(BLK // SLOT, SLOT, model), axis=0)
            dsec = norm_back(dy, unit2, s2, gain_f)
            dlow = dsec.astype(bf16)
            db[r, :] = dlow
            backs = []
            for g in range(groups):
                total = jnp.zeros((BLK, WIDTH), f32)
                for k in range(plan.shards // part):
                    da = dg(dlow[:, g * WIDTH:(g + 1) * WIDTH], weight("outer%d" % g, k), 1, 1)
                    at = g * nff + k * da.shape[1]
                    di = (da * slope[:, at:at + da.shape[1]].astype(f32)).astype(bf16)
                    dinner[r, at:at + da.shape[1]] = di
                    total = total + dg(di, weight("inter%d" % g, k), 1, 0)
                backs.append(total)
            dn = dsec + jnp.concatenate(backs, axis=1)
            gn[AUG + SLOT:AUG + 2 * SLOT, :] += jnp.sum((dn * unit1).reshape(BLK // SLOT, SLOT, model), axis=0)
            dfirst = norm_back(dn, unit1, s1, gain_a)
            hg[r, :] = dfirst
            do = dfirst.astype(bf16)
            dout[r, :] = do
        blocks(mid)

        for g in range(groups):
            cols = slice(g * WIDTH, (g + 1) * WIDTH)
            for slot, (name, left, right) in enumerate((("outer", act, db), ("inter", dinner, nl))):
                drain(slot)
                for k in range(4):
                    n = nff // 4
                    at = g * nff + k * n
                    stage[slot, k * n:(k + 1) * n, :] = dg(left[:, at:at + n], right[:, cols], 0, 0).astype(bf16)
                outgoing("%s%d" % (name, g), slot).start()
                send[slot] = "%s%d" % (name, g)

    ff = 2 * plan.rows_ff * plan.shards
    pl.run_scoped(
        mid_scope,
        pltpu.VMEM((length, ff), bf16),
        pltpu.VMEM((length, ff), bf16),
        pltpu.VMEM((length, model), bf16),
        pltpu.VMEM((length, model), bf16),
        pltpu.VMEM((BLK, ff), bf16),
    )

    def back_scope(xf, doaT, dS, dall, dkc, dlog, dcv, prod, gd):
        for j in range(groups):
            ship("out%d" % j, dg(ctx[...], dout[:, j * WIDTH:(j + 1) * WIDTH], 0, 0), j % 2)

        def dctx(b):
            r = rows_of(b)
            d = dout[r, :]
            full = sum(
                dg(d[:, j * WIDTH:(j + 1) * WIDTH], weight("out%d" % j), 1, 1) for j in range(groups)
            ).astype(bf16)
            ctx[r, att:] = full[:, att:]
            dT = full[:, 0:att].T.astype(f32)
            for h in range(heads):
                scaled = (dT[h * hs:(h + 1) * hs] * linv[h:h + 1, r]).astype(bf16)
                doaT[h, 0:hs, r] = scaled
                drop = -jnp.sum(scaled.astype(f32) * attT[h * hs:(h + 1) * hs, r], axis=0, keepdims=True)
                d1 = drop.astype(bf16).astype(f32)
                d2 = (drop - d1).astype(bf16).astype(f32)
                d3 = drop - d1 - d2
                line = lax.broadcasted_iota(jnp.int32, (AUG, BLK), 0)
                extra = jnp.where(line == 0, d1, jnp.where(line == 1, d2, jnp.where(line == 2, d3, 0.0)))
                doaT[h, hs:, r] = extra.astype(bf16)
        blocks(dctx)

        order = [heads - 2, heads - 1] + list(range(heads - 2))

        def p_in(h, slot):
            return pltpu.make_async_copy(probs_hbm.at[h], prob.at[slot], dsem.at[len(names) + slot])

        for i, h in enumerate(order):
            slot = i % 2 if heads % 2 == 0 else (heads - 2 + i) % 2
            if i >= 2:
                p_in(h, slot).wait()

            def bwd(b, h=h, slot=slot):
                r = rows_of(b)
                dp = dg(doaT[h, :, r], vaT[h], 0, 0)
                dS[r, :] = (prob[slot, r, :].astype(f32) * dp).astype(bf16)
            blocks(bwd)
            dqT = dg(kaT[h, 0:hs, :], dS[...], 1, 1) * (hs ** -0.5)
            dkT = dg(qaT[h, 0:hs, :], dS[...], 1, 0)
            dvT = dg(doaT[h, 0:hs, :], prob[slot], 1, 0)
            attT[h * hs:(h + 1) * hs, :] = dqT
            kaT[h, 0:hs, :] = dkT.astype(bf16)
            vaT[h, 0:hs, :] = dvT.astype(bf16)
            if i + 2 < heads:
                p_in(order[i + 2], slot).start()

        pad_edges(xf)
        for c in range(cols_a):
            dcv[c, :, :] = jnp.zeros((length + 2 * PADR, LANES), f32)

        def conv_back(b, carry):
            base = pl.multiple_of(b * CV, CV)
            r = pl.ds(base, CV)
            w = tw[r, :]
            mask = cmf[r, :]
            pair = split(w * mask)
            dt = jnp.zeros((CV, LANES), f32)
            for c in range(cols_a):
                dc = ctx[r, att + c * LANES:att + (c + 1) * LANES].astype(f32)
                big = dg(pair, expand[:, c * span:(c + 1) * span], 1, 0)
                for t in range(taps):
                    at = base + PADR + t - half
                    prod[:, t * LANES:(t + 1) * LANES] = (dc * cvf[c, pl.ds(at, CV), :]).astype(bf16)
                    dcv[c, pl.ds(at, CV), :] += big[:, t * LANES:(t + 1) * LANES] * dc
                dt = dt + dg(prod[...], expand[0:LANES, c * span:(c + 1) * span], 1, 1)
            dt = dt * mask
            total = dt * w
            for s in (64, 32, 16, 8):
                total = total + pltpu.roll(total, b * 0 + s, 1)
            dl = (w * (dt - total)).astype(bf16)
            dlog[r, :] = dl
            dm = dg(dl, wkT, 1, 1).astype(bf16).astype(f32)
            dkc[r, :] = (dm * qs[r, :].astype(f32)).astype(bf16)
            kc[r, :] = dm * kc[r, :]
            return carry
        lax.fori_loop(0, length // CV, conv_back, 0)

        def collect(b):
            r = rows_of(b)
            at = pl.multiple_of(b * BLK, BLK) + PADR
            dall[r, 0:att] = (attT[:, r].T + kc[r, :]).astype(bf16)
            for h in range(heads):
                pass
            kk = jnp.concatenate([kaT[h, 0:hs, r] for h in range(heads)], axis=0)
            vv = jnp.concatenate([vaT[h, 0:hs, r] for h in range(heads)], axis=0)
            dall[r, att:2 * att] = kk.T
            dall[r, 2 * att:3 * att] = vv.T
            for c in range(cols_a):
                dall[r, 3 * att + c * LANES:3 * att + (c + 1) * LANES] = dcv[c, pl.ds(at, BLK), :].astype(bf16)
            dd = dg(dkc[r, :], weight("keyconv"), 1, 1).astype(bf16).astype(f32)
            for c in range(cols_m):
                xf[c, pl.ds(at, BLK), :] = dd[:, c * LANES:(c + 1) * LANES]
            total = hg[r, :]
            for j, name in enumerate(("query", "key", "value", "convout")):
                total = total + dg(dall[r, j * att:(j + 1) * att], weight(name), 1, 1)
            hg[r, :] = total
        blocks(collect)

        ship("keyconv", dg(depth_low[...], dkc[...], 0, 0), 0)
        for j, name in enumerate(("query", "key", "value", "convout")):
            ship(name, dg(hid[...], dall[:, j * att:(j + 1) * att], 0, 0), (j + 1) % 2)

        gk = dg(mixed[...], dlog[...], 0, 0)

        gd[...] = jnp.zeros(gd.shape, f32)

        def depth_back(b, carry):
            base = pl.multiple_of(b * CH, CH)
            own = segb[pl.ds(base + PADR, CH), :]
            r = pl.ds(base, CH)
            sames = [segb[pl.ds(base + PADR + t - half, CH), :] == own for t in range(taps)]
            for c in range(cols_m):
                lanes = slice(c * LANES, (c + 1) * LANES)
                x = hid[r, lanes].astype(f32)
                acc = hg[r, lanes]
                for t in range(taps):
                    back = taps - 1 - t
                    v = jnp.where(sames[t], xf[c, pl.ds(base + PADR + t - half, CH), :], 0.0)
                    acc = acc + v * gn[back:back + 1, lanes]
                    gd[back, :, lanes] += jnp.sum((v * x).reshape(CH // SLOT, SLOT, LANES), axis=0)
                hg[r, lanes] = acc
            return carry
        lax.fori_loop(0, length // CH, depth_back, 0)

        rows = [jnp.sum(gd[t], axis=0, keepdims=True) for t in range(taps)]
        rows.append(jnp.sum(gn[AUG + SLOT:AUG + 2 * SLOT, :], axis=0, keepdims=True))
        rows.append(jnp.sum(gn[AUG:AUG + SLOT, :], axis=0, keepdims=True))
        rows.append(jnp.zeros((LANES - len(rows), model), f32))
        pf = jnp.concatenate(rows, axis=0).T
        slot = 0
        drain(slot)
        nr = plan.rows_small
        for s in range(plan.shards):
            parts = [gk[s * ns:(s + 1) * ns]] + [
                pf[(2 * s + j) * ns:(2 * s + j + 1) * ns] for j in range(2)
            ]
            piece = jnp.concatenate(parts, axis=1)
            if nr > ns:
                piece = jnp.concatenate([piece, jnp.zeros((nr - ns, WIDTH), f32)], axis=0)
            stage[slot, s * nr:(s + 1) * nr, :] = piece.astype(bf16)
        outgoing("small", slot).start()
        send[slot] = "small"
        for slot in sorted(send):
            drain(slot)

    pl.run_scoped(
        back_scope,
        pltpu.VMEM((cols_m, length + 2 * PADR, LANES), f32),
        pltpu.VMEM((heads, hs + AUG, length), bf16),
        pltpu.VMEM((length, length), bf16),
        pltpu.VMEM((length, 4 * att), bf16),
        pltpu.VMEM((length, att), bf16),
        pltpu.VMEM((length, LANES), bf16),
        pltpu.VMEM((cols_a, length + 2 * PADR, LANES), f32),
        pltpu.VMEM((CV, span), bf16),
        pltpu.VMEM((taps, SLOT, model), f32),
    )


def run_mega(plan, heads, taps, hidden, cotangent, segr, gath):
    length, model = hidden.shape
    att = WIDTH
    hs = att // heads
    cols_m, cols_a = model // LANES, att // LANES
    names = [n for n in plan.offset if n != "small"]
    sh = plan.shards
    big = sh * max(plan.rows_in, plan.rows_ff)

    def body(hid, cot, sg, ga, o, h, gr, ph, *rest):
        nw = len(names)
        wts = dict(zip(names, rest[:nw]))
        mega(plan, heads, taps, length, model, hid, cot, sg, ga, o, h, gr, ph, wts, *rest[nw:])

    vm = pl.BlockSpec(memory_space=pltpu.VMEM)
    an = pl.BlockSpec(memory_space=pl.ANY)
    return pl.pallas_call(
        body,
        out_shape=(
            jax.ShapeDtypeStruct((length, model), bf16),
            jax.ShapeDtypeStruct((length, model), f32),
            jax.ShapeDtypeStruct((sh, plan.rows, WIDTH), bf16),
            jax.ShapeDtypeStruct((heads, length, length), bf16),
        ),
        in_specs=[vm, vm, vm, an],
        out_specs=(vm, vm, an, an),
        scratch_shapes=[pltpu.VMEM((sh, plan.count[n], WIDTH), bf16) for n in names]
        + [
            pltpu.VMEM((sh, plan.rows_small, WIDTH), bf16),
            pltpu.VMEM((length + 16, LANES), f32),
            pltpu.VMEM((length, LANES), f32),
            pltpu.VMEM((heads, hs + AUG, length), bf16),
            pltpu.VMEM((heads, hs + AUG, length), bf16),
            pltpu.VMEM((heads, hs + AUG, length), bf16),
            pltpu.VMEM((length, att), bf16),
            pltpu.VMEM((cols_a, length + 16, LANES), f32),
            pltpu.VMEM((length, LANES), f32),
            pltpu.VMEM((length, model), bf16),
            pltpu.VMEM((length, att), f32),
            pltpu.VMEM((length, att), bf16),
            pltpu.VMEM((length, 2 * att), bf16),
            pltpu.VMEM((att, length), f32),
            pltpu.VMEM((SLOT, length), f32),
            pltpu.VMEM((2, length, length), bf16),
            pltpu.VMEM((2 * LANES, cols_a * taps * LANES), bf16),
            pltpu.VMEM((AUG + 2 * SLOT, model), f32),
            pltpu.VMEM((length, model), bf16),
            pltpu.VMEM((2, big, WIDTH), bf16),
            pltpu.SemaphoreType.DMA((len(plan.offset) + 4,)),
        ],
        compiler_params=pltpu.CompilerParams(vmem_limit_bytes=67043328),
    )(hidden, cotangent, segr, gath)


def pack(plan, taps, w_query, w_key, w_value, w_depth, w_keyconv, w_kernel, w_convout, w_output, gain_attn, w_inter, w_outer, gain_ffn):
    ns = plan.n_small
    heads = w_kernel.shape[0] // taps
    wk = w_kernel.reshape(heads, taps, ns).transpose(2, 1, 0)
    wk = jnp.pad(wk, ((0, 0), (0, 0), (0, SLOT - heads))).reshape(ns, taps * SLOT)
    wk = jnp.pad(wk, ((0, 0), (0, LANES - taps * SLOT)))
    pf = jnp.concatenate([w_depth, gain_attn[None], gain_ffn[None]], axis=0).T
    pf = jnp.pad(pf, ((0, 0), (0, LANES - pf.shape[1])))
    small = jnp.concatenate([wk, pf[:ns], pf[ns:]], axis=1)
    small = jnp.pad(small, ((0, plan.rows_small - ns), (0, 0)))
    groups = w_inter.shape[0]
    values = dict(query=w_query, key=w_key, value=w_value, keyconv=w_keyconv, convout=w_convout, small=small)
    for g in range(groups):
        values["out%d" % g] = w_output[:, g * WIDTH:(g + 1) * WIDTH]
        values["inter%d" % g] = w_inter[g].T
        values["outer%d" % g] = w_outer[g]
    parts = []
    at = 0
    for name, start in plan.offset.items():
        if start > at:
            parts.append(jnp.zeros((start - at, WIDTH), bf16))
        parts.append(values[name])
        at = start + plan.count[name]
    if plan.rows > at:
        parts.append(jnp.zeros((plan.rows - at, WIDTH), bf16))
    return jnp.concatenate(parts, axis=0)


def unpack(plan, taps, heads, groups, total):
    ns, rin, rff = plan.n_small, plan.rows_in, plan.rows_ff
    model = rin * plan.shards

    def body(src, gq, gkey, gv, gd, gkc, gker, gco, gout, gga, gin, gou, ggf):
        def part(name):
            return src[plan.offset[name]:plan.offset[name] + plan.count[name], :].astype(f32)
        for name, ref in (("query", gq), ("key", gkey), ("value", gv), ("keyconv", gkc), ("convout", gco)):
            ref[...] = part(name)
        for j in range(groups):
            gout[:, j * WIDTH:(j + 1) * WIDTH] = part("out%d" % j)
            gin[j] = part("inter%d" % j).T
            gou[j] = part("outer%d" % j)
        small = part("small")[:ns]
        turned = small[:, 0:LANES].T
        for h in range(heads):
            for t in range(taps):
                gker[h * taps + t:h * taps + t + 1, :] = turned[t * SLOT + h:t * SLOT + h + 1]
        pf = jnp.concatenate([small[:, LANES:2 * LANES], small[:, 2 * LANES:]], axis=0).T
        gd[...] = pf[0:taps]
        gga[...] = pf[taps:taps + 1]
        ggf[...] = pf[taps + 1:taps + 2]

    def out(*dims):
        return jax.ShapeDtypeStruct(dims, f32)
    square = out(rin, WIDTH)
    parts = list(pl.pallas_call(
        body,
        out_shape=(
            square, square, square, out(taps, rin), square, out(heads * taps, ns), square, out(rin, model),
            out(1, rin), out(groups, WIDTH, rff), out(groups, rff, WIDTH), out(1, rin),
        ),
    )(total))
    for i in (8, 11):
        parts[i] = parts[i].reshape(rin)
    return tuple(parts)


class Place:
    def __init__(self, reps, shards):
        side = math.isqrt(reps)
        self.sy, self.sx = (side, side) if side * side == reps else (1, reps)
        self.cores = 2 if shards % 2 == 0 else 1
        self.nz = shards // self.cores
        self.reps = reps
        self.shard = lax.axis_index("shard")
        self.rep = lax.axis_index("rep")
        self.z = self.shard // self.cores
        self.core = self.shard % self.cores
        self.py = self.rep // self.sx
        self.px = self.rep % self.sx

    def at_x(self, d):
        return lax.rem(self.px + d, self.sx)

    def at_y(self, d):
        return lax.rem(self.py + d, self.sy)

    def id(self, rep=None, shard=None):
        return {
            "rep": self.rep if rep is None else rep,
            "shard": self.shard if shard is None else shard,
        }

    def xpeer(self, d):
        return self.id(rep=self.py * self.sx + self.at_x(d))

    def ypeer(self, d):
        return self.id(rep=self.at_y(d) * self.sx + self.px)

    def partner(self):
        return self.id(shard=self.z * self.cores + (1 - self.core))

    def right(self):
        return self.id(shard=self.shard + self.cores)

    def left(self):
        return self.id(shard=self.shard - self.cores)

    def barrier(self):
        sem = pltpu.get_barrier_semaphore()

        def hello(device):
            pl.semaphore_signal(sem, inc=1, device_id=device, device_id_type=pl.DeviceIdType.MESH)

        for d in range(1, self.sx):
            hello(self.xpeer(d))
        for d in range(1, self.sy):
            hello(self.ypeer(d))
        if self.cores == 2:
            hello(self.partner())
        pl.when(self.z > 0)(lambda: hello(self.left()))
        pl.when(self.z < self.nz - 1)(lambda: hello(self.right()))
        steady = self.sx + self.sy - 2 + self.cores - 1
        ends = jnp.where(self.z > 0, 1, 0) + jnp.where(self.z < self.nz - 1, 1, 0)
        pl.semaphore_wait(sem, steady + ends)


def remote(src, dst, send, recv, device):
    return pltpu.make_async_remote_copy(
        src_ref=src, dst_ref=dst, send_sem=send, recv_sem=recv,
        device_id=device, device_id_type=pl.DeviceIdType.MESH,
    )


class Gather:
    def __init__(self, place, base, chunk, own, full, sems):
        self.p, self.base, self.chunk, self.own, self.full = place, base, chunk, own, full
        self.item, self.zsend, self.share = sems
        self.ha = up(chunk // 2, 16)

    @staticmethod
    def sems(place_dims):
        reps, nz = place_dims
        return [
            pltpu.SemaphoreType.DMA((nz, reps, 2)),
            pltpu.SemaphoreType.DMA((2, nz)),
            pltpu.SemaphoreType.DMA((4,)),
        ]

    def rows(self, q, half=None):
        start = self.base + q * self.chunk
        if half is None:
            return pl.ds(pl.multiple_of(start, 16), self.chunk)
        if half == 0:
            return pl.ds(pl.multiple_of(start, 16), self.ha)
        return pl.ds(pl.multiple_of(start + self.ha, 16), self.chunk - self.ha)

    def move(self, zs, q, half, send, recv, device, src=None):
        at = self.full.at[zs * self.p.cores + self.p.core, self.rows(q, half)]
        return remote(at if src is None else src, at, send, recv, device)

    def plane(self, zs, q, half, device, which):
        self.move(zs, q, half, self.share.at[0], self.item.at[zs, q, which], device).start()

    def hand(self, zs, q):
        if self.p.cores == 2:
            self.move(zs, q, None, self.share.at[1], self.share.at[2], self.p.partner()).start()

    def arrived(self, zs, q, half, which):
        self.move(zs, q, half, self.share.at[0], self.item.at[zs, q, which], self.p.partner()).wait_recv()

    def start(self):
        p = self.p
        mine = self.own.at[self.rows(p.rep)]
        pl.when(p.z < p.nz - 1)(lambda: self.move(
            p.z, p.rep, None, self.zsend.at[0, 0], self.item.at[p.z, p.rep, 0], p.right(), mine).start())
        pl.when(p.z > 0)(lambda: self.move(
            p.z, p.rep, None, self.zsend.at[1, 0], self.item.at[p.z, p.rep, 0], p.left(), mine).start())
        if p.cores == 2:
            self.whole(p.partner()).start()
        self.keep().start()

    def whole(self, device):
        r = pl.ds(self.base, self.p.reps * self.chunk)
        return remote(self.own.at[r], self.full.at[self.p.shard, r], self.share.at[1], self.share.at[2], device)

    def keep(self):
        r = pl.ds(self.base, self.p.reps * self.chunk)
        return pltpu.make_async_copy(self.own.at[r], self.full.at[self.p.shard, r], self.share.at[3])

    def both(self, k, body):
        p = self.p
        pl.when(p.z - k >= 0)(lambda: body(p.z - k, 0))
        pl.when(p.z + k < p.nz)(lambda: body(p.z + k, 1))

    def along(self, k):
        p = self.p

        def body(zs, way):
            self.arrived(zs, p.rep, None, 0)
            more = p.z < p.nz - 1 if way == 0 else p.z > 0
            pl.when(more)(lambda: self.move(
                zs, p.rep, None, self.zsend.at[way, k], self.item.at[zs, p.rep, 0],
                p.right() if way == 0 else p.left()).start())
            for d in range(1, p.sx):
                self.plane(zs, p.rep, None, p.xpeer(d), 0)
            for d in range(1, p.sy):
                self.plane(zs, p.rep, None, p.ypeer(d), 0)
            self.hand(zs, p.rep)
        self.both(k, body)

    def across(self, k):
        p = self.p

        def body(zs, way):
            for d in range(1, p.sx):
                q = p.py * p.sx + p.at_x(d)
                self.arrived(zs, q, None, 0)
                for e in range(1, p.sy):
                    self.plane(zs, q, 0, p.ypeer(e), 0)
                self.hand(zs, q)
            for d in range(1, p.sy):
                q = p.at_y(d) * p.sx + p.px
                self.arrived(zs, q, None, 0)
                for e in range(1, p.sx):
                    self.plane(zs, q, 1, p.xpeer(e), 1)
                self.hand(zs, q)
        self.both(k, body)

    def corner(self, k):
        p = self.p

        def body(zs, way):
            for d in range(1, p.sy):
                for e in range(1, p.sx):
                    q = p.at_y(d) * p.sx + p.at_x(e)
                    self.arrived(zs, q, 0, 0)
                    self.arrived(zs, q, 1, 1)
                    self.hand(zs, q)
        self.both(k, body)

    def finish(self):
        p = self.p
        self.keep().wait()
        if p.cores == 2:
            r = self.full.at[pl.ds(0, p.nz), pl.ds(self.base, p.reps * self.chunk)]
            both = remote(r, r, self.share.at[1], self.share.at[2], p.partner())
            both.wait_recv()
            both.wait_send()
        if p.nz > 1 and p.reps > 1:
            r = self.full.at[pl.ds(0, p.nz - 1), pl.ds(0, (p.reps - 1) * self.chunk)]
            remote(r, r, self.share.at[0], self.share.at[2], p.partner()).wait_send()
        for way in range(2):
            for k in range(p.nz - 1):
                if way == 0:
                    sent = (p.z - k >= 0) & (p.z < p.nz - 1)
                else:
                    sent = (p.z + k < p.nz) & (p.z > 0)
                pl.when(sent)(lambda way=way, k=k: self.move(
                    p.z, p.rep, None, self.zsend.at[way, k], self.share.at[2], p.partner()).wait_send())


def chunk_of(rows, reps):
    return up(-(-rows // reps), 16)


class Reduce:
    def __init__(self, place, chunk, src, land, bufs, done, sems):
        self.p, self.chunk, self.src, self.land, self.done = place, chunk, src, land, done
        self.xa, self.yb, self.ya, self.xb, self.zr, self.zl = bufs
        self.near, self.sx, self.sy, self.s2x, self.s2y, self.zin, self.fin, self.out = sems
        self.ha = up(chunk // 2, 16)
        p = place
        self.order = []
        lo, hi = 0, p.nz - 1
        while lo <= hi:
            self.order.append(hi)
            if lo < hi:
                self.order.append(lo)
            lo, hi = lo + 1, hi - 1

    @staticmethod
    def buffers(reps, shards, chunk):
        side = math.isqrt(reps)
        sy, sx = (side, side) if side * side == reps else (1, reps)
        nz = shards // (2 if shards % 2 == 0 else 1)
        ha = up(chunk // 2, 16)
        hb = chunk - ha
        dx, dy = max(sx - 1, 1), max(sy - 1, 1)
        return [
            pltpu.VMEM((dx, nz, sy, ha, WIDTH), bf16),
            pltpu.VMEM((dy, nz, sx, hb, WIDTH), bf16),
            pltpu.VMEM((dy, nz, ha, WIDTH), bf16),
            pltpu.VMEM((dx, nz, hb, WIDTH), bf16),
            pltpu.VMEM((nz, chunk, WIDTH), bf16),
            pltpu.VMEM((nz, chunk, WIDTH), bf16),
        ]

    @staticmethod
    def sems(reps, shards):
        side = math.isqrt(reps)
        sy, sx = (side, side) if side * side == reps else (1, reps)
        nz = shards // (2 if shards % 2 == 0 else 1)
        dx, dy = max(sx - 1, 1), max(sy - 1, 1)
        dma = pltpu.SemaphoreType.DMA
        return [
            dma((nz,)), dma((dx, nz)), dma((dy, nz)), dma((dx, nz)), dma((dy, nz)),
            dma((2, nz)), dma((sy, sx, 2)), dma((7,)),
        ]

    def rows(self, q, half=None):
        start = q * self.chunk
        if half is None:
            return pl.ds(pl.multiple_of(start, 16), self.chunk)
        if half == 0:
            return pl.ds(pl.multiple_of(start, 16), self.ha)
        return pl.ds(pl.multiple_of(start + self.ha, 16), self.chunk - self.ha)

    def to_partner(self, zd, device):
        other = zd * self.p.cores + (1 - self.p.core)
        return remote(self.src(other), self.land.at[zd], self.out.at[0], self.near.at[zd], device)

    def start(self):
        for zd in self.order:
            self.to_partner(zd, self.p.partner()).start()

    def tiles(self, body, n):
        step = 16
        def one(i, carry):
            body(pl.multiple_of(i * step, step), step)
            return carry
        lax.fori_loop(0, n // step, one, 0)

    def add_into(self, ref, start, n, others):
        def body(i, step):
            r = pl.ds(pl.multiple_of(start + i, 16), step)
            total = ref[r, :].astype(f32)
            for other in others:
                total = total + other[pl.ds(i, step), :].astype(f32)
            ref[r, :] = total.astype(bf16)
        self.tiles(body, n)

    def cores(self, zd, own):
        p = self.p
        self.to_partner(zd, p.partner()).wait_recv()
        self.add_into(self.land.at[zd], 0, p.reps * self.chunk, [own(zd)])
        for d in range(1, p.sx):
            for y in range(p.sy):
                remote(
                    self.land.at[zd, self.rows(y * p.sx + p.at_x(d), 0)],
                    self.xa.at[p.sx - d - 1, zd, y],
                    self.out.at[1], self.sx.at[p.sx - d - 1, zd], p.xpeer(d),
                ).start()
        for d in range(1, p.sy):
            for x in range(p.sx):
                remote(
                    self.land.at[zd, self.rows(p.at_y(d) * p.sx + x, 1)],
                    self.yb.at[p.sy - d - 1, zd, x],
                    self.out.at[2], self.sy.at[p.sy - d - 1, zd], p.ypeer(d),
                ).start()

    def first(self, zd):
        p = self.p
        here = self.land.at[zd]
        for d in range(p.sx - 1):
            remote(self.xa.at[d, zd], self.xa.at[d, zd], self.out.at[1], self.sx.at[d, zd], p.partner()).wait_recv()
        for d in range(p.sy - 1):
            remote(self.yb.at[d, zd], self.yb.at[d, zd], self.out.at[2], self.sy.at[d, zd], p.partner()).wait_recv()
        for y in range(p.sy):
            if p.sx > 1:
                self.add_into(here, (y * p.sx + p.px) * self.chunk, self.ha, [self.xa.at[d, zd, y] for d in range(p.sx - 1)])
        for x in range(p.sx):
            if p.sy > 1:
                self.add_into(here, (p.py * p.sx + x) * self.chunk + self.ha, self.chunk - self.ha, [self.yb.at[d, zd, x] for d in range(p.sy - 1)])
        for d in range(1, p.sy):
            remote(
                self.land.at[zd, self.rows(p.at_y(d) * p.sx + p.px, 0)],
                self.ya.at[p.sy - d - 1, zd],
                self.out.at[3], self.s2y.at[p.sy - d - 1, zd], p.ypeer(d),
            ).start()
        for d in range(1, p.sx):
            remote(
                self.land.at[zd, self.rows(p.py * p.sx + p.at_x(d), 1)],
                self.xb.at[p.sx - d - 1, zd],
                self.out.at[4], self.s2x.at[p.sx - d - 1, zd], p.xpeer(d),
            ).start()

    def second(self, zd):
        p = self.p
        here = self.land.at[zd]
        for d in range(p.sy - 1):
            remote(self.ya.at[d, zd], self.ya.at[d, zd], self.out.at[3], self.s2y.at[d, zd], p.partner()).wait_recv()
        for d in range(p.sx - 1):
            remote(self.xb.at[d, zd], self.xb.at[d, zd], self.out.at[4], self.s2x.at[d, zd], p.partner()).wait_recv()
        if p.sy > 1:
            self.add_into(here, p.rep * self.chunk, self.ha, [self.ya.at[d, zd] for d in range(p.sy - 1)])
        if p.sx > 1:
            self.add_into(here, p.rep * self.chunk + self.ha, self.chunk - self.ha, [self.xb.at[d, zd] for d in range(p.sx - 1)])

    def hop(self, zd, way):
        buf = self.zr if way == 0 else self.zl
        return remote(
            self.land.at[zd, self.rows(self.p.rep)], buf.at[zd], self.out.at[5], self.zin.at[way, zd],
            self.p.right() if way == 0 else self.p.left(),
        )

    def line(self, zd):
        p = self.p
        here = self.land.at[zd]

        def go(way, inner):
            def more():
                self.hop(zd, way).wait_recv()
                self.add_into(here, p.rep * self.chunk, self.chunk, [(self.zr if way == 0 else self.zl).at[zd]])
            pl.when(inner)(more)
            self.hop(zd, way).start()
        pl.when(zd > p.z)(lambda: go(0, p.z > 0))
        pl.when(zd < p.z)(lambda: go(1, p.z < p.nz - 1))

    def total(self):
        p = self.p
        for way, there in ((0, p.z > 0), (1, p.z < p.nz - 1)):
            def more(way=way):
                self.hop(p.z, way).wait_recv()
                self.add_into(self.land.at[p.z], p.rep * self.chunk, self.chunk, [(self.zr if way == 0 else self.zl).at[p.z]])
            pl.when(there)(more)

        def copy(i, step):
            r = pl.ds(pl.multiple_of(p.rep * self.chunk + i, 16), step)
            self.done[r, :] = self.land[p.z, r, :]
        self.tiles(copy, self.chunk)
        for d in range(1, p.sx):
            self.spread(p.rep, None, p.xpeer(d), 0, p.sx - d, 0).start()
        for d in range(1, p.sy):
            self.spread(p.rep, None, p.ypeer(d), p.sy - d, 0, 0).start()

    def spread(self, q, half, device, dy, dx, which):
        at = self.done.at[self.rows(q, half)]
        return remote(at, at, self.out.at[6], self.fin.at[dy, dx, which], device)

    def around(self):
        p = self.p
        for d in range(1, p.sx):
            q = p.py * p.sx + p.at_x(d)
            self.spread(q, None, p.partner(), 0, d, 0).wait_recv()
            for e in range(1, p.sy):
                self.spread(q, 0, p.ypeer(e), p.sy - e, d, 0).start()
        for d in range(1, p.sy):
            q = p.at_y(d) * p.sx + p.px
            self.spread(q, None, p.partner(), d, 0, 0).wait_recv()
            for e in range(1, p.sx):
                self.spread(q, 1, p.xpeer(e), d, p.sx - e, 1).start()

    def finish(self):
        p = self.p
        for d in range(1, p.sy):
            for e in range(1, p.sx):
                q = p.at_y(d) * p.sx + p.at_x(e)
                self.spread(q, 0, p.partner(), d, e, 0).wait_recv()
                self.spread(q, 1, p.partner(), d, e, 1).wait_recv()

        def sent(ref, i):
            remote(ref, ref, self.out.at[i], self.near.at[0], p.partner()).wait_send()
        sent(self.land, 0)
        if p.sx > 1:
            sent(self.xa, 1)
            sent(self.xb, 4)
        if p.sy > 1:
            sent(self.yb, 2)
            sent(self.ya, 3)
        if p.nz > 1:
            sent(self.zr.at[pl.ds(0, p.nz - 1)], 5)
        if p.reps > 1:
            sent(self.done.at[pl.ds(0, (p.reps - 1) * self.chunk)], 6)


def run_gather(reps, shards, own, chunks):
    rows = own.shape[0]
    nz = shards // (2 if shards % 2 == 0 else 1)

    def body(own_ref, full, *sems):
        place = Place(reps, shards)
        place.barrier()
        parts = []
        base = 0
        for i, chunk in enumerate(chunks):
            parts.append(Gather(place, base, chunk, own_ref, full, sems[3 * i:3 * i + 3]))
            base += reps * chunk
        for g in parts:
            g.start()
        for g in parts:
            for k in range(1, place.nz):
                g.along(k)
            for k in range(1, place.nz):
                g.across(k)
        for g in parts:
            for k in range(1, place.nz):
                g.corner(k)
        for g in parts:
            g.finish()

    return pl.pallas_call(
        body,
        out_shape=jax.ShapeDtypeStruct((shards, rows, WIDTH), bf16),
        in_specs=[pl.BlockSpec(memory_space=pltpu.VMEM)],
        out_specs=pl.BlockSpec(memory_space=pl.ANY),
        scratch_shapes=[s for _ in chunks for s in Gather.sems((reps, nz))],
        compiler_params=pltpu.CompilerParams(collective_id=1, has_side_effects=True),
    )(own)


def run_reduce(reps, shards, grads):
    rows = grads.shape[1]
    chunk = rows // reps
    cores = 2 if shards % 2 == 0 else 1
    nz = shards // cores
    nbuf = 6

    def body(src, done, land, own, *rest):
        place = Place(reps, shards)
        bufs, sems, local = rest[:nbuf], rest[nbuf:-1], rest[-1]
        red = Reduce(place, chunk, lambda s: src.at[s], land, bufs, done, sems)

        def fetch(zd):
            return pltpu.make_async_copy(src.at[zd * cores + place.core], own.at[zd], local.at[zd])
        for zd in red.order:
            fetch(zd).start()
        place.barrier()
        red.start()
        for zd in red.order:
            fetch(zd).wait()
            red.cores(zd, lambda zd: own.at[zd])
        for zd in red.order:
            red.first(zd)
        for zd in red.order:
            red.second(zd)
            red.line(zd)
        red.total()
        red.around()
        red.finish()

    return pl.pallas_call(
        body,
        out_shape=jax.ShapeDtypeStruct((rows, WIDTH), bf16),
        in_specs=[pl.BlockSpec(memory_space=pl.ANY)],
        out_specs=pl.BlockSpec(memory_space=pltpu.VMEM),
        scratch_shapes=[pltpu.VMEM((nz, rows, WIDTH), bf16), pltpu.VMEM((nz, rows, WIDTH), bf16)]
        + Reduce.buffers(reps, shards, chunk) + Reduce.sems(reps, shards) + [pltpu.SemaphoreType.DMA((nz,))],
        compiler_params=pltpu.CompilerParams(collective_id=2, has_side_effects=True, vmem_limit_bytes=60 << 20),
    )(grads)


def local(hidden, segment_ids, cotangent, *weights):
    w_query, w_depth, w_kernel, w_inter, w_outer = weights[0], weights[3], weights[5], weights[9], weights[10]
    shards, reps = lax.axis_size("shard"), lax.axis_size("rep")
    taps = w_depth.shape[0]
    heads = w_kernel.shape[0] // taps
    groups = w_inter.shape[0]
    model = hidden.shape[1]
    plan = Plan(reps, shards, model, w_query.shape[1], w_outer.shape[1] * shards, groups)
    packed = pack(plan, taps, *weights)
    gathered = run_gather(reps, shards, packed, plan.chunks)
    output, hidden_grad, grads, _ = run_mega(plan, heads, taps, hidden, cotangent, segment_ids, gathered)
    total = run_reduce(reps, shards, grads)
    return (output, hidden_grad, *unpack(plan, taps, heads, groups, total))


def solution(mesh):
    both = P(("rep", "shard"), None)
    rows = P("shard", None)
    cols = P(None, "shard")
    params = (
        rows, rows, rows, cols, rows, cols, rows, rows, P("shard"),
        P(None, None, "shard"), P(None, "shard", None), P("shard"),
    )
    return jax.shard_map(
        local, mesh=mesh, in_specs=(both, both, both) + params, out_specs=(both, both) + params, check_vma=False
    )
```
